32 devices in a mesh: cuts: 2 (over x), mode: 8 (over z, y), branch: 2 (over core).
Axes of the slice: x: 2, y: 2, z: 4, core: 2. Of those that a mesh axis runs over, the one named last changes fastest.
Arguments:
- leaves: bfloat16 [8, 2, 32, 512, 512], P('branch', None, ('cuts', 'mode')), parts along dimension 2, may hold values from -0.1875 to 0.1875
- join_order: int32 [7], replicated, may hold values from 0 to 1
- slice_values: int32 [32], P(('cuts', 'mode')), parts along dimension 0, may hold values from 0 to 1
- boundary: bfloat16 [2, 2, 512, 512], replicated, may hold values from -4 to 4
Outputs:
- amplitudes: float32 [2, 32, 512, 512], P(None, ('cuts', 'mode'), 'branch'), parts along dimension 1
The draws below stay inside these ranges and needn't reach their ends.
There are 2 independent parts, one for each index of `cuts`. The reference program is written for one: setup_inputs(seed, part) draws one part's arguments, and reference() takes and returns one part's arrays. A program takes and returns all parts, laid end to end along the dimension named above; an argument that names none is the same for every part. Nothing has to cross between parts.
Inputs may be any that keep to these rules, and one draw needn't show every extreme that they name: `join_order`: 1 puts the second operand of the join on the left.
All inputs are finite; a program needn't handle non-finite values.
Results may differ from the reference program's by a relative error of at most 0.0076.
Values may be sent and summed in bfloat16 or wider, within the bound.
A program may use at most 64 MiB of HBM per device.

```python
import jax
import jax.numpy as jnp
from jax import lax

M = 512
LEAVES = 8
BOND = 2
BATCH = 16
N_MODE = 8


def with_ends(values, own_key, smallest, largest):
    extent = values.shape
    index_at = [jax.random.randint(jax.random.fold_in(own_key, axis), (), 0, extent[axis]) for axis in range(len(extent))]
    values = values.at[tuple(index_at)].set(smallest)
    longest = extent.index(max(extent))
    index_at[longest] = (index_at[longest] + 1) % extent[longest]
    return values.at[tuple(index_at)].set(largest)


def block_levels(own_key, extent, split, smallest, largest):
    def one(position, blocks):
        draws = jax.random.uniform(jax.random.fold_in(jax.random.fold_in(own_key, 6), position), (blocks,), jnp.float32, smallest / len(split), largest / len(split))
        return jnp.repeat(jnp.exp(draws), extent[position] // blocks).reshape((-1,) + (1,) * (len(extent) - position - 1))

    factor_of = one(*split[0])
    for cut in split[1:]:
        factor_of = factor_of * one(*cut)
    return factor_of


def bell_draw(own_key, shape, deviation, most, split=(), kind=jnp.bfloat16):
    array = deviation * jax.random.normal(own_key, shape, jnp.float32)
    if split:
        array = array * block_levels(own_key, shape, split, -0.22, 0.18)
    return jnp.clip(array, -most, most).astype(kind)


def setup_inputs(seed: int = 0, part: int = 0) -> dict:
    streams_of = jax.random.split(jax.random.key(seed), 5)
    own_keys = jax.random.split(jax.random.fold_in(streams_of[4], part), 5)
    leaves = bell_draw(own_keys[0], (LEAVES, 2, BATCH, M, M), (2 * M) ** -0.5, 0.1875, ((0, 2), (2, 8)))
    join_order = with_ends(jax.random.randint(streams_of[1], (LEAVES - 1,), 0, 2), jax.random.fold_in(streams_of[1], 1), 0, 1).astype(jnp.int32)
    slice_values = with_ends(jax.random.randint(own_keys[2], (BATCH,), 0, BOND), jax.random.fold_in(own_keys[2], 1), 0, BOND - 1).astype(jnp.int32)
    boundary = bell_draw(streams_of[3], (BOND, 2, M, M), 0.7, 4.0)
    return {"leaves": leaves, "join_order": join_order, "slice_values": slice_values, "boundary": boundary}


def complex_sums(left_op, right_op):
    spec = "bij,bjk->bik"
    left_real = left_op[0].astype(jnp.float32)
    left_imag = left_op[1].astype(jnp.float32)
    right_real = right_op[0].astype(jnp.float32)
    right_imag = right_op[1].astype(jnp.float32)
    real_part = jnp.einsum(spec, left_real, right_real) - jnp.einsum(spec, left_imag, right_imag)
    imag_part = jnp.einsum(spec, left_real, right_imag) + jnp.einsum(spec, left_imag, right_real)
    return jnp.stack([real_part, imag_part])


def complex_product(left_op, right_op):
    return complex_sums(left_op, right_op).astype(jnp.bfloat16)


def join_pair(left_op, right_op, swapped):
    return lax.cond(swapped == 1, lambda: complex_product(right_op, left_op), lambda: complex_product(left_op, right_op))


def reorder_rows(tensor):
    blocks = N_MODE
    block_rows = M // blocks
    viewed = tensor.reshape(2, BATCH, blocks, block_rows, M)
    return jnp.transpose(viewed, (0, 2, 1, 3, 4)).reshape(2, BATCH, M, M)


def reference(leaves, join_order, slice_values, boundary):
    first_level = []
    for index in range(4):
        joined = join_pair(leaves[2 * index], leaves[2 * index + 1], join_order[index])
        first_level.append(reorder_rows(joined))
    second_level = []
    for index in range(2):
        joined = join_pair(first_level[2 * index], first_level[2 * index + 1], join_order[4 + index])
        second_level.append(reorder_rows(joined))
    top_tensor = join_pair(second_level[0], second_level[1], join_order[6])
    chosen = jnp.where(slice_values[None, :, None, None] == 1, boundary[1][:, None], boundary[0][:, None])
    return complex_sums(top_tensor, chosen).astype(jnp.float32)
```

```python
import functools

import jax
import jax.numpy as jnp
from jax import lax
from jax.experimental import pallas as pl
from jax.experimental.pallas import tpu as pltpu
from jax.sharding import PartitionSpec as P

MESH = pl.DeviceIdType.MESH


def dot(left, right):
    return jnp.dot(left, right, preferred_element_type=jnp.float32)


def complex_rows(left_real, left_imag, right_real, right_imag):
    real_part = dot(left_real, right_real) - dot(left_imag, right_imag)
    imag_part = dot(left_real, right_imag) + dot(left_imag, right_real)
    return real_part, imag_part


def contract_kernel(
    per, order_ref, slices_ref, leaves_ref, boundary_ref, out_ref,
    prod, right, left, result, chosen,
    leaf_sem, own_right, own_left,
    cross_right_send, cross_right_recv, cross_left_send, cross_left_recv,
    column_send, column_recv, relay_send, relay_recv,
    deliver_send, deliver_recv, forward_send, forward_recv, chosen_sem, *blocks_of,
):
    leaf, middle = blocks_of[:per], blocks_of[per:]
    n = lax.axis_size("mode")
    group = n // per
    pair = 2
    peers = group // pair
    rounds = n // pair
    wide = pair * per
    m = lax.axis_index("mode")
    core = lax.axis_index("branch")
    h, g = m // group, lax.rem(m, group)
    line, side = g // pair, lax.rem(g, pair)
    across = pair * line + 1 - side
    blk, width = prod.shape[-2:]
    order = n * blk
    outer = lax.rem(line + h + 1, 2) == 1

    def remote(src, dst, send, recv, **device):
        return pltpu.make_async_remote_copy(
            src_ref=src,
            dst_ref=dst,
            send_sem=send,
            recv_sem=recv,
            device_id=device,
            device_id_type=MESH,
        )

    def column(line_at):
        return pair * line_at + side

    def up(k):
        return lax.rem(line + k, peers)

    def down(k):
        return lax.rem(line + peers - k, peers)

    def own_right_copy(q, e):
        return pltpu.make_async_copy(
            prod.at[0, :, e, pair * q + side], right.at[q, :, per * g + e], own_right.at[q, e]
        )

    def own_left_copy(q, e):
        return pltpu.make_async_copy(
            prod.at[1, :, e, pair * q + side], left.at[q, :, per * side + e], own_left.at[q, e]
        )

    def cross_right(q, e, source=None):
        return remote(
            prod.at[0, :, e, pair * q + 1 - side],
            right.at[q, :, per * (g if source is None else source) + e],
            cross_right_send.at[q, e],
            cross_right_recv.at[q, e],
            mode=h * group + across,
        )

    def cross_left(q, e, source=None):
        return remote(
            prod.at[1, :, e, pair * q + 1 - side],
            left.at[q, :, per * (side if source is None else source) + e],
            cross_left_send.at[q, e],
            cross_left_recv.at[q, e],
            mode=h * group + across,
        )

    def column_right(q, e, k, target, source):
        return remote(
            prod.at[0, :, e, pair * q + side],
            right.at[q, :, per * column(source) + e],
            column_send.at[q, e, k],
            column_recv.at[q, e, k],
            mode=h * group + column(target),
        )

    def relay_right(q, e, k, target, source):
        part = right.at[q, :, per * (pair * source + 1 - side) + e]
        return remote(
            part,
            part,
            relay_send.at[q, e, k],
            relay_recv.at[q, e, k],
            mode=h * group + column(target),
        )

    def entry(q):
        return wide * q // n

    def row_of(q, h_from, side_from):
        return lax.rem(wide * q + per * side_from + h_from, n)

    def deliver(q, i):
        return remote(
            result.at[q, :, i],
            middle[entry(q)].at[core, :, row_of(q, h, side)],
            deliver_send.at[q, i],
            deliver_recv.at[q, pair * h + side],
            mode=wide * line + i,
        )

    def deliver_own(q, i):
        return pltpu.make_async_copy(
            result.at[q, :, i],
            middle[entry(q)].at[core, :, row_of(q, h, side)],
            deliver_recv.at[q, pair * h + side],
        )

    def delivered(q, h_from, side_from):
        part = middle[entry(q)].at[core, :, row_of(q, h_from, side_from)]
        return pltpu.make_async_copy(part, part, deliver_recv.at[q, pair * h_from + side_from])

    def forward(q, h_from, side_from, owner):
        part = middle[entry(q)].at[owner, :, row_of(q, h_from, side_from)]
        at = pair * h_from + side_from
        return remote(
            part, part, forward_send.at[q, at], forward_recv.at[q, at], branch=1 - core
        )

    def leaf_copy(e):
        return pltpu.make_async_copy(leaves_ref.at[:, :, e], leaf[e], leaf_sem.at[e])

    middle_order = order_ref[4 + core]
    tile = min(256, order)

    def first_tile(slot, e, step):
        which = 1 - middle_order if slot == 0 else middle_order
        flag = order_ref[2 * core + which]
        left_leaf = 2 * which + flag
        right_leaf = 2 * which + 1 - flag
        at = pl.ds(pl.multiple_of(step * tile, tile), tile)
        real_part, imag_part = complex_rows(
            leaf[e][left_leaf, 0, at, :],
            leaf[e][left_leaf, 1, at, :],
            leaf[e][right_leaf, 0],
            leaf[e][right_leaf, 1],
        )
        blocks = tile // blk
        shape = (blocks, blk, width)
        to = pl.ds(step * blocks, blocks)
        prod[slot, 0, e, to] = real_part.astype(prod.dtype).reshape(shape)
        prod[slot, 1, e, to] = imag_part.astype(prod.dtype).reshape(shape)

    def later_tiles(slot, e):
        @pl.loop(1, order // tile)
        def _(step):
            first_tile(slot, e, step)

    def send_cross_right(q):
        for e in range(per):
            cross_right(q, e).start()

    def send_cross_left(q):
        for e in range(per):
            cross_left(q, e).start()
            own_left_copy(q, e).start()

    def send_column(q, e):
        for k in range(1, peers):
            column_right(q, e, k, up(k), line).start()
        own_right_copy(q, e).start()

    def send_relay(q, e):
        cross_right(q, e, across).wait_recv()
        for k in range(1, peers):
            relay_right(q, e, k, up(k), line).start()

    def relay_round(q):
        for e in range(per):
            send_column(q, e)
        for e in range(per):
            send_relay(q, e)

    def send_result(q, i):
        here = wide * line + i == m

        @pl.when(jnp.logical_not(here))
        def _():
            deliver(q, i).start()

        @pl.when(here)
        def _():
            deliver_own(q, i).start()

    def near(q):
        near_pair = lax.rem(line + h + 1, 2)
        for t in range(pair):
            send_result(q, near_pair * (pair * h + t) + (1 - near_pair) * (pair * t + side))

    def far(q):
        near_pair = lax.rem(line + h + 1, 2)
        for t in range(pair):
            send_result(
                q,
                near_pair * (pair * (1 - h) + t) + (1 - near_pair) * (pair * t + 1 - side),
            )

    row_tile = wide * blk

    def join_round(q):
        for e in range(per):
            own_right_copy(q, e).wait()
            own_left_copy(q, e).wait()
            cross_left(q, e, 1 - side).wait_recv()
            for k in range(1, peers):
                column_right(q, e, k, down(k), down(k)).wait_recv()
                relay_right(q, e, k, down(k), down(k)).wait_recv()

        real_part, imag_part = complex_rows(
            left[q, 0].reshape(row_tile, width),
            left[q, 1].reshape(row_tile, width),
            right[q, 0].reshape(order, width),
            right[q, 1].reshape(order, width),
        )
        result[q, 0] = real_part.astype(result.dtype).reshape(wide, blk, width)
        result[q, 1] = imag_part.astype(result.dtype).reshape(wide, blk, width)

    def top_entry(b):
        rows, half = n // 2, order // 2
        last = order_ref[order_ref.shape[0] - 1]
        at = pl.ds(core * rows, rows)
        value = slices_ref[b]
        top_real, top_imag = complex_rows(
            middle[b][last, 0, at].reshape(half, width),
            middle[b][last, 1, at].reshape(half, width),
            middle[b][1 - last, 0].reshape(order, width),
            middle[b][1 - last, 1].reshape(order, width),
        )
        real_part, imag_part = complex_rows(
            top_real.astype(prod.dtype),
            top_imag.astype(prod.dtype),
            chosen[value, 0],
            chosen[value, 1],
        )
        out_ref[0, b] = real_part
        out_ref[1, b] = imag_part

    barrier = pltpu.get_barrier_semaphore()
    for k in range(1, n):
        pl.semaphore_signal(
            barrier, inc=1, device_id={"mode": lax.rem(m + k, n)}, device_id_type=MESH
        )
    pl.semaphore_signal(barrier, inc=1, device_id={"branch": 1 - core}, device_id_type=MESH)
    for e in range(per):
        leaf_copy(e).start()
    boundary_copy = pltpu.make_async_copy(boundary_ref, chosen, chosen_sem)

    for e in range(per):
        leaf_copy(e).wait()
        first_tile(0, e, 0)
        if e == 0:
            pl.semaphore_wait(barrier, n)
        cross_right(0, e).start()
        send_column(0, e)
    for e in range(per):
        first_tile(1, e, 0)
        cross_left(0, e).start()
        own_left_copy(0, e).start()
    boundary_copy.start()
    for e in range(per):
        send_relay(0, e)
        later_tiles(0, e)
    for q in range(1, min(3, rounds)):
        send_cross_right(q)
    for e in range(per):
        later_tiles(1, e)
    for q in range(1, rounds):
        send_cross_left(q)
        if q + 2 < rounds:
            send_cross_right(q + 2)

    join_round(0)
    near(0)
    far(0)
    for q in range(1, min(3, rounds)):
        relay_round(q)
    for q in range(1, rounds):
        join_round(q)
        near(q)
        far(q)
        if q + 2 < rounds:
            relay_round(q + 2)

    boundary_copy.wait()
    for b in range(per):
        mine = [q for q in range(rounds) if entry(q) == b]
        sources = [(h_from, side_from) for h_from in range(per) for side_from in range(pair)]
        for q in mine:
            for h_from, side_from in sources:
                delivered(q, h_from, side_from).wait()
                forward(q, h_from, side_from, core).start()
        for q in mine:
            for h_from, side_from in sources:
                forward(q, h_from, side_from, 1 - core).wait_recv()
        top_entry(b)

    for q in range(rounds):
        for e in range(per):
            cross_right(q, e).wait_send()
            cross_left(q, e).wait_send()
            for k in range(1, peers):
                column_right(q, e, k, up(k), line).wait_send()
                relay_right(q, e, k, up(k), line).wait_send()
        for i in range(wide):

            @pl.when(wide * line + i != m)
            def _():
                deliver(q, i).wait_send()

        for h_from in range(per):
            for side_from in range(pair):
                forward(q, h_from, side_from, core).wait_send()


def contract(leaves, join_order, slice_values, boundary):
    n = lax.axis_size("mode")
    count, _, per, order, width = leaves.shape
    blk = order // n
    rounds, peers, wide = n // 2, n // per // 2, 2 * per
    dma = pltpu.SemaphoreType.DMA
    dtype = leaves.dtype
    return pl.pallas_call(
        functools.partial(contract_kernel, per),
        out_shape=jax.ShapeDtypeStruct((2, per, order // 2, width), jnp.float32),
        in_specs=[
            pl.BlockSpec(memory_space=pltpu.SMEM),
            pl.BlockSpec(memory_space=pltpu.SMEM),
            pl.BlockSpec(memory_space=pl.ANY),
            pl.BlockSpec(memory_space=pl.ANY),
        ],
        out_specs=pl.BlockSpec(memory_space=pltpu.VMEM),
        scratch_shapes=[
            pltpu.VMEM((2, 2, per, n, blk, width), dtype),
            pltpu.VMEM((rounds, 2, n, blk, width), dtype),
            pltpu.VMEM((rounds, 2, wide, blk, width), dtype),
            pltpu.VMEM((rounds, 2, wide, blk, width), dtype),
            pltpu.VMEM(boundary.shape, dtype),
            dma((per,)),
            dma((rounds, per)),
            dma((rounds, per)),
            dma((rounds, per)),
            dma((rounds, per)),
            dma((rounds, per)),
            dma((rounds, per)),
            dma((rounds, per, peers)),
            dma((rounds, per, peers)),
            dma((rounds, per, peers)),
            dma((rounds, per, peers)),
            dma((rounds, wide)),
            dma((rounds, wide)),
            dma((rounds, wide)),
            dma((rounds, wide)),
            dma(()),
        ]
        + [pltpu.VMEM((count, 2, order, width), dtype)] * per
        + [pltpu.VMEM((2, 2, n, blk, width), dtype)] * per,
        compiler_params=pltpu.CompilerParams(
            collective_id=0, has_side_effects=True, vmem_limit_bytes=58 << 20
        ),
        name="contract",
    )(join_order, slice_values, leaves, boundary)


def per_device(leaves, join_order, slice_values, boundary):
    return contract(leaves, join_order, slice_values, boundary)


def solution(mesh):
    in_specs = (P("branch", None, ("cuts", "mode"), None, None), P(), P(("cuts", "mode")), P())
    out_specs = P(None, ("cuts", "mode"), "branch", None)
    return jax.shard_map(
        per_device, mesh=mesh, in_specs=in_specs, out_specs=out_specs, check_vma=False
    )
```

```python
import functools

import jax
import jax.numpy as jnp
from jax import lax
from jax.experimental import pallas as pl
from jax.experimental.pallas import tpu as pltpu
from jax.sharding import PartitionSpec as P

MESH = pl.DeviceIdType.MESH


def dot(left, right):
    return jnp.dot(left, right, preferred_element_type=jnp.float32)


def complex_rows(left_real, left_imag, right_real, right_imag):
    real_part = dot(left_real, right_real) - dot(left_imag, right_imag)
    imag_part = dot(left_real, right_imag) + dot(left_imag, right_real)
    return real_part, imag_part


OUTER = (("C", -2), ("Xb", 2), ("R", -7), ("Oa", 1), ("Y", -2), ("Ob", 2), ("Xa", 1), ("L", -3))
INNER = (("Xb", 3), ("Oa", 1), ("Xa", 2), ("R", -2), ("Ob", 2), ("Y", 0), ("L", -2), ("C", -3))


def schedule(lags, rounds):
    steps = [[] for _ in range(2 * rounds + 1)]
    for move, lag in lags:
        for q in range(1 if move in "RLCY" else 0, rounds):
            steps[min(max(2 * q + lag, 0), 2 * rounds)].append((move, q))
    return steps


def contract_kernel(
    per, order_ref, slices_ref, leaves_ref, boundary_ref, out_ref,
    prod, right, left, result, chosen,
    leaf_sem, own_right,
    cross_right_send, cross_right_recv, cross_left_send, cross_left_recv,
    column_send, column_recv, relay_send, relay_recv,
    deliver_send, deliver_recv,
    forward_send, forward_recv, chosen_sem, *blocks_of,
):
    leaf, middle = blocks_of[:per], blocks_of[per:]
    n = lax.axis_size("mode")
    group = n // per
    pair = 2
    peers = group // pair
    rounds = n // pair
    wide = pair * per
    m = lax.axis_index("mode")
    core = lax.axis_index("branch")
    h, g = m // group, lax.rem(m, group)
    line, side = g // pair, lax.rem(g, pair)
    across = pair * line + 1 - side
    blk, width = prod.shape[-2:]
    order = n * blk
    outer = lax.rem(line + h + 1, 2) == 1

    def remote(src, dst, send, recv, **device):
        return pltpu.make_async_remote_copy(
            src_ref=src,
            dst_ref=dst,
            send_sem=send,
            recv_sem=recv,
            device_id=device,
            device_id_type=MESH,
        )

    def column(line_at):
        return pair * line_at + side

    def up(k):
        return lax.rem(line + k, peers)

    def down(k):
        return lax.rem(line + peers - k, peers)

    def own_right_copy(q, e):
        return pltpu.make_async_copy(
            prod.at[0, :, e, pair * q + side], right.at[q, :, per * g + e], own_right.at[q, e]
        )

    def cross_right(q, e, source=None):
        return remote(
            prod.at[0, :, e, pair * q + 1 - side],
            right.at[q, :, per * (g if source is None else source) + e],
            cross_right_send.at[q, e],
            cross_right_recv.at[q, e],
            mode=h * group + across,
        )

    def cross_left(q, e):
        return remote(
            prod.at[1, :, e, pair * q + 1 - side],
            left.at[q, :, e],
            cross_left_send.at[q, e],
            cross_left_recv.at[q, e],
            mode=h * group + across,
        )

    def column_right(q, e, k, target, source):
        return remote(
            prod.at[0, :, e, pair * q + side],
            right.at[q, :, per * column(source) + e],
            column_send.at[q, e, k],
            column_recv.at[q, e, k],
            mode=h * group + column(target),
        )

    def relay_right(q, e, k, target, source):
        part = right.at[q, :, per * (pair * source + 1 - side) + e]
        return remote(
            part,
            part,
            relay_send.at[q, e, k],
            relay_recv.at[q, e, k],
            mode=h * group + column(target),
        )

    def entry(q):
        return wide * q // n

    def row_of(q, h_from, side_from):
        return lax.rem(wide * q + per * side_from + h_from, n)

    def straight(origin, t):
        return per * origin + pair * t + side

    def crossing(origin, t):
        return per * origin + pair * t + 1 - side

    def deliver(q, i):
        return remote(
            result.at[q, :, i],
            middle[entry(q)].at[core, :, row_of(q, h, side)],
            deliver_send.at[q, i],
            deliver_recv.at[q, pair * h + side],
            mode=wide * line + i,
        )

    def deliver_own(q, i):
        return pltpu.make_async_copy(
            result.at[q, :, i],
            middle[entry(q)].at[core, :, row_of(q, h, side)],
            deliver_recv.at[q, pair * h + side],
        )

    def delivered(q, h_from, side_from):
        part = middle[entry(q)].at[core, :, row_of(q, h_from, side_from)]
        return pltpu.make_async_copy(part, part, deliver_recv.at[q, pair * h_from + side_from])

    def forward(q, h_from, side_from, owner):
        part = middle[entry(q)].at[owner, :, row_of(q, h_from, side_from)]
        at = pair * h_from + side_from
        return remote(
            part, part, forward_send.at[q, at], forward_recv.at[q, at], branch=1 - core
        )

    def leaf_copy(e):
        return pltpu.make_async_copy(leaves_ref.at[:, :, e], leaf[e], leaf_sem.at[e])

    middle_order = order_ref[4 + core]
    tile = min(128, order)

    def first_tile(slot, e, step):
        which = 1 - middle_order if slot == 0 else middle_order
        flag = order_ref[2 * core + which]
        left_leaf = 2 * which + flag
        right_leaf = 2 * which + 1 - flag
        at = pl.ds(pl.multiple_of(step * tile, tile), tile)
        real_part, imag_part = complex_rows(
            leaf[e][left_leaf, 0, at, :],
            leaf[e][left_leaf, 1, at, :],
            leaf[e][right_leaf, 0],
            leaf[e][right_leaf, 1],
        )
        blocks = tile // blk
        shape = (blocks, blk, width)
        to = pl.ds(step * blocks, blocks)
        prod[slot, 0, e, to] = real_part.astype(prod.dtype).reshape(shape)
        prod[slot, 1, e, to] = imag_part.astype(prod.dtype).reshape(shape)

    def later_tiles(slot, e):
        @pl.loop(1, order // tile)
        def _(step):
            first_tile(slot, e, step)

    def send_cross_right(q):
        for e in range(per):
            cross_right(q, e).start()

    def send_cross_left(q):
        for e in range(per):
            cross_left(q, e).start()

    def send_column(q):
        for e in range(per):
            for k in range(1, peers):
                column_right(q, e, k, up(k), line).start()
            own_right_copy(q, e).start()

    def send_relay(q, e):
        cross_right(q, e, across).wait_recv()
        for k in range(1, peers):
            relay_right(q, e, k, up(k), line).start()

    def send_relays(q):
        for e in range(per):
            send_relay(q, e)

    def send_straight(q, origin):
        for t in range(per // pair):
            i = straight(origin, t)
            here = wide * line + i == m

            @pl.when(jnp.logical_not(here))
            def _():
                deliver(q, i).start()

            @pl.when(here)
            def _():
                deliver_own(q, i).start()

    def send_crossing(q, origin):
        for t in range(per // pair):
            deliver(q, crossing(origin, t)).start()

    rows_of = per * blk

    def second_join(q, origin, left_real, left_imag):
        real_part, imag_part = complex_rows(
            left_real.reshape(rows_of, width),
            left_imag.reshape(rows_of, width),
            right[q, 0].reshape(order, width),
            right[q, 1].reshape(order, width),
        )
        to = pl.ds(per * origin, per)
        result[q, 0, to] = real_part.astype(result.dtype).reshape(per, blk, width)
        result[q, 1, to] = imag_part.astype(result.dtype).reshape(per, blk, width)

    def join_own(q):
        for e in range(per):
            own_right_copy(q, e).wait()
            for k in range(1, peers):
                column_right(q, e, k, down(k), down(k)).wait_recv()
                relay_right(q, e, k, down(k), down(k)).wait_recv()
        at = pair * q + side
        second_join(q, side, prod[1, 0, :, at], prod[1, 1, :, at])

    def join_across(q):
        for e in range(per):
            cross_left(q, e).wait_recv()
        second_join(q, 1 - side, left[q, 0], left[q, 1])

    def top_entry(b):
        rows, half = n // 2, order // 2
        last = order_ref[order_ref.shape[0] - 1]
        at = pl.ds(core * rows, rows)
        value = slices_ref[b]
        top_real, top_imag = complex_rows(
            middle[b][last, 0, at].reshape(half, width),
            middle[b][last, 1, at].reshape(half, width),
            middle[b][1 - last, 0].reshape(order, width),
            middle[b][1 - last, 1].reshape(order, width),
        )
        real_part, imag_part = complex_rows(
            top_real.astype(prod.dtype),
            top_imag.astype(prod.dtype),
            chosen[value, 0],
            chosen[value, 1],
        )
        out_ref[0, b] = real_part
        out_ref[1, b] = imag_part

    boundary_copy = pltpu.make_async_copy(boundary_ref, chosen, chosen_sem)
    for e in range(per):
        leaf_copy(e).start()
    barrier = pltpu.get_barrier_semaphore()
    for k in range(1, n):
        pl.semaphore_signal(
            barrier, inc=1, device_id={"mode": lax.rem(m + k, n)}, device_id_type=MESH
        )
    pl.semaphore_signal(barrier, inc=1, device_id={"branch": 1 - core}, device_id_type=MESH)

    for e in range(per):
        leaf_copy(e).wait()
        first_tile(0, e, 0)
        if e == 0:
            pl.semaphore_wait(barrier, n)
        cross_right(0, e).start()
        for k in range(1, peers):
            column_right(0, e, k, up(k), line).start()
        own_right_copy(0, e).start()
    for e in range(per):
        first_tile(1, e, 0)
        cross_left(0, e).start()
    boundary_copy.start()
    for e in range(per):
        send_relay(0, e)
        later_tiles(0, e)
    for e in range(per):
        later_tiles(1, e)

    moves = {
        "R": send_cross_right,
        "L": send_cross_left,
        "C": send_column,
        "Y": send_relays,
        "Oa": lambda q: send_straight(q, side),
        "Ob": lambda q: send_straight(q, 1 - side),
        "Xa": lambda q: send_crossing(q, side),
        "Xb": lambda q: send_crossing(q, 1 - side),
    }

    def run(steps):
        for move, q in steps:
            moves[move](q)

    outer_steps, inner_steps = schedule(OUTER, rounds), schedule(INNER, rounds)
    for step in range(2 * rounds + 1):
        if outer_steps[step] == inner_steps[step]:
            run(outer_steps[step])
        else:

            @pl.when(outer)
            def _():
                run(outer_steps[step])

            @pl.when(jnp.logical_not(outer))
            def _():
                run(inner_steps[step])

        if step < 2 * rounds:
            (join_across if step % 2 else join_own)(step // 2)

    boundary_copy.wait()
    for b in range(per):
        mine = [q for q in range(rounds) if entry(q) == b]
        sources = [(h_from, side_from) for h_from in range(per) for side_from in range(pair)]
        for q in mine:
            for h_from, side_from in sources:
                delivered(q, h_from, side_from).wait()
                forward(q, h_from, side_from, core).start()
        for q in mine:
            for h_from, side_from in sources:
                forward(q, h_from, side_from, 1 - core).wait_recv()
        top_entry(b)

    for q in range(rounds):
        for e in range(per):
            cross_right(q, e).wait_send()
            cross_left(q, e).wait_send()
            for k in range(1, peers):
                column_right(q, e, k, up(k), line).wait_send()
                relay_right(q, e, k, up(k), line).wait_send()
        for i in range(wide):

            @pl.when(wide * line + i != m)
            def _():
                deliver(q, i).wait_send()

        for h_from in range(per):
            for side_from in range(pair):
                forward(q, h_from, side_from, core).wait_send()


def contract(leaves, join_order, slice_values, boundary):
    n = lax.axis_size("mode")
    count, _, per, order, width = leaves.shape
    blk = order // n
    rounds, peers, wide = n // 2, n // per // 2, 2 * per
    dma = pltpu.SemaphoreType.DMA
    dtype = leaves.dtype
    return pl.pallas_call(
        functools.partial(contract_kernel, per),
        out_shape=jax.ShapeDtypeStruct((2, per, order // 2, width), jnp.float32),
        in_specs=[
            pl.BlockSpec(memory_space=pltpu.SMEM),
            pl.BlockSpec(memory_space=pltpu.SMEM),
            pl.BlockSpec(memory_space=pltpu.HBM),
            pl.BlockSpec(memory_space=pltpu.HBM),
        ],
        out_specs=pl.BlockSpec(memory_space=pltpu.VMEM),
        scratch_shapes=[
            pltpu.VMEM((2, 2, per, n, blk, width), dtype),
            pltpu.VMEM((rounds, 2, n, blk, width), dtype),
            pltpu.VMEM((rounds, 2, per, blk, width), dtype),
            pltpu.VMEM((rounds, 2, wide, blk, width), dtype),
            pltpu.VMEM(boundary.shape, dtype),
            dma((per,)),
            dma((rounds, per)),
            dma((rounds, per)),
            dma((rounds, per)),
            dma((rounds, per)),
            dma((rounds, per)),
            dma((rounds, per, peers)),
            dma((rounds, per, peers)),
            dma((rounds, per, peers)),
            dma((rounds, per, peers)),
            dma((rounds, wide)),
            dma((rounds, wide)),
            dma((rounds, wide)),
            dma((rounds, wide)),
            dma(()),
        ]
        + [pltpu.VMEM((count, 2, order, width), dtype)] * per
        + [pltpu.VMEM((2, 2, n, blk, width), dtype)] * per,
        compiler_params=pltpu.CompilerParams(
            collective_id=0, has_side_effects=True, vmem_limit_bytes=48 << 20
        ),
        name="contract",
    )(
        pltpu.with_memory_space_constraint(join_order, pltpu.HBM),
        pltpu.with_memory_space_constraint(slice_values, pltpu.HBM),
        pltpu.with_memory_space_constraint(leaves, pltpu.HBM),
        pltpu.with_memory_space_constraint(boundary, pltpu.HBM),
    )


def per_device(leaves, join_order, slice_values, boundary):
    return contract(leaves, join_order, slice_values, boundary)


def solution(mesh):
    in_specs = (P("branch", None, ("cuts", "mode"), None, None), P(), P(("cuts", "mode")), P())
    out_specs = P(None, ("cuts", "mode"), "branch", None)
    return jax.shard_map(
        per_device, mesh=mesh, in_specs=in_specs, out_specs=out_specs, check_vma=False
    )
```

```python
import functools

import jax
import jax.numpy as jnp
from jax import lax
from jax.experimental import pallas as pl
from jax.experimental.pallas import tpu as pltpu
from jax.sharding import PartitionSpec as P

MESH = pl.DeviceIdType.MESH


def dot(left, right):
    return jnp.dot(left, right, preferred_element_type=jnp.float32)


def complex_rows(left_real, left_imag, right_real, right_imag):
    real_part = dot(left_real, right_real) - dot(left_imag, right_imag)
    imag_part = dot(left_real, right_imag) + dot(left_imag, right_real)
    return real_part, imag_part


OUTER = (("C", -2), ("Xb", 2), ("R", -7), ("Oa", 1), ("Y", -2), ("Ob", 2), ("Xa", 1), ("L", -3))
INNER = (("Xb", 3), ("Oa", 1), ("Xa", 2), ("R", -2), ("Ob", 2), ("Y", 0), ("L", -2), ("C", -3))


def schedule(lags, rounds):
    steps = [[] for _ in range(2 * rounds + 1)]
    for move, lag in lags:
        for q in range(1 if move in "RLCY" else 0, rounds):
            steps[min(max(2 * q + lag, 0), 2 * rounds)].append((move, q))
    return steps


def contract_kernel(
    per, order_ref, slices_ref, leaves_ref, boundary_ref, out_ref,
    prod, right, left, result, chosen,
    leaf_sem, own_right,
    cross_right_send, cross_right_recv, cross_left_send, cross_left_recv,
    column_send, column_recv, relay_send, relay_recv,
    deliver_send, deliver_recv,
    forward_send, forward_recv, chosen_sem, *blocks_of,
):
    leaf, middle = blocks_of[:per], blocks_of[per:]
    n = lax.axis_size("mode")
    group = n // per
    pair = 2
    peers = group // pair
    rounds = n // pair
    wide = pair * per
    m = lax.axis_index("mode")
    core = lax.axis_index("branch")
    h, g = m // group, lax.rem(m, group)
    line, side = g // pair, lax.rem(g, pair)
    across = pair * line + 1 - side
    blk, width = prod.shape[-2:]
    order = n * blk
    outer = lax.rem(line + h + 1, 2) == 1

    def remote(src, dst, send, recv, **device):
        return pltpu.make_async_remote_copy(
            src_ref=src,
            dst_ref=dst,
            send_sem=send,
            recv_sem=recv,
            device_id=device,
            device_id_type=MESH,
        )

    def column(line_at):
        return pair * line_at + side

    def up(k):
        return lax.rem(line + k, peers)

    def down(k):
        return lax.rem(line + peers - k, peers)

    def own_right_copy(q, e):
        return pltpu.make_async_copy(
            prod.at[0, :, e, pair * q + side], right.at[q, :, per * g + e], own_right.at[q, e]
        )

    def cross_right(q, e, source=None):
        return remote(
            prod.at[0, :, e, pair * q + 1 - side],
            right.at[q, :, per * (g if source is None else source) + e],
            cross_right_send.at[q, e],
            cross_right_recv.at[q, e],
            mode=h * group + across,
        )

    def cross_left(q, e):
        return remote(
            prod.at[1, :, e, pair * q + 1 - side],
            left.at[q, :, e],
            cross_left_send.at[q, e],
            cross_left_recv.at[q, e],
            mode=h * group + across,
        )

    def column_right(q, e, k, target, source):
        return remote(
            prod.at[0, :, e, pair * q + side],
            right.at[q, :, per * column(source) + e],
            column_send.at[q, e, k],
            column_recv.at[q, e, k],
            mode=h * group + column(target),
        )

    def relay_right(q, e, k, target, source):
        part = right.at[q, :, per * (pair * source + 1 - side) + e]
        return remote(
            part,
            part,
            relay_send.at[q, e, k],
            relay_recv.at[q, e, k],
            mode=h * group + column(target),
        )

    def entry(q):
        return wide * q // n

    def row_of(q, h_from, side_from):
        return lax.rem(wide * q + per * side_from + h_from, n)

    def straight(origin, t):
        return per * origin + pair * t + side

    def crossing(origin, t):
        return per * origin + pair * t + 1 - side

    def deliver(q, i):
        return remote(
            result.at[q, :, i],
            middle[entry(q)].at[core, :, row_of(q, h, side)],
            deliver_send.at[q, i],
            deliver_recv.at[q, pair * h + side],
            mode=wide * line + i,
        )

    def deliver_own(q, i):
        return pltpu.make_async_copy(
            result.at[q, :, i],
            middle[entry(q)].at[core, :, row_of(q, h, side)],
            deliver_recv.at[q, pair * h + side],
        )

    def delivered(q, h_from, side_from):
        part = middle[entry(q)].at[core, :, row_of(q, h_from, side_from)]
        return pltpu.make_async_copy(part, part, deliver_recv.at[q, pair * h_from + side_from])

    def forward(q, h_from, side_from, owner):
        part = middle[entry(q)].at[owner, :, row_of(q, h_from, side_from)]
        at = pair * h_from + side_from
        return remote(
            part, part, forward_send.at[q, at], forward_recv.at[q, at], branch=1 - core
        )

    def leaf_copy(e):
        return pltpu.make_async_copy(leaves_ref.at[:, :, e], leaf[e], leaf_sem.at[e])

    middle_order = order_ref[4 + core]
    tile = min(128, order)

    def first_tile(slot, e, step):
        which = 1 - middle_order if slot == 0 else middle_order
        flag = order_ref[2 * core + which]
        left_leaf = 2 * which + flag
        right_leaf = 2 * which + 1 - flag
        at = pl.ds(pl.multiple_of(step * tile, tile), tile)
        real_part, imag_part = complex_rows(
            leaf[e][left_leaf, 0, at, :],
            leaf[e][left_leaf, 1, at, :],
            leaf[e][right_leaf, 0],
            leaf[e][right_leaf, 1],
        )
        blocks = tile // blk
        shape = (blocks, blk, width)
        to = pl.ds(step * blocks, blocks)
        prod[slot, 0, e, to] = real_part.astype(prod.dtype).reshape(shape)
        prod[slot, 1, e, to] = imag_part.astype(prod.dtype).reshape(shape)

    def later_tiles(slot, e):
        @pl.loop(1, order // tile)
        def _(step):
            first_tile(slot, e, step)

    def send_cross_right(q):
        for e in range(per):
            cross_right(q, e).start()

    def send_cross_left(q):
        for e in range(per):
            cross_left(q, e).start()

    def send_column(q):
        for e in range(per):
            for k in range(1, peers):
                column_right(q, e, k, up(k), line).start()
            own_right_copy(q, e).start()

    def send_relay(q, e):
        cross_right(q, e, across).wait_recv()
        for k in range(1, peers):
            relay_right(q, e, k, up(k), line).start()

    def send_relays(q):
        for e in range(per):
            send_relay(q, e)

    def send_straight(q, origin):
        for t in range(per // pair):
            i = straight(origin, t)
            here = wide * line + i == m

            @pl.when(jnp.logical_not(here))
            def _():
                deliver(q, i).start()

            @pl.when(here)
            def _():
                deliver_own(q, i).start()

    def send_crossing(q, origin):
        for t in range(per // pair):
            deliver(q, crossing(origin, t)).start()

    rows_of = per * blk

    def second_join(q, origin, left_real, left_imag):
        real_part, imag_part = complex_rows(
            left_real.reshape(rows_of, width),
            left_imag.reshape(rows_of, width),
            right[q, 0].reshape(order, width),
            right[q, 1].reshape(order, width),
        )
        to = pl.ds(per * origin, per)
        result[q, 0, to] = real_part.astype(result.dtype).reshape(per, blk, width)
        result[q, 1, to] = imag_part.astype(result.dtype).reshape(per, blk, width)

    def join_own(q):
        for e in range(per):
            own_right_copy(q, e).wait()
            for k in range(1, peers):
                column_right(q, e, k, down(k), down(k)).wait_recv()
                relay_right(q, e, k, down(k), down(k)).wait_recv()
        at = pair * q + side
        second_join(q, side, prod[1, 0, :, at], prod[1, 1, :, at])

    def join_across(q):
        for e in range(per):
            cross_left(q, e).wait_recv()
        second_join(q, 1 - side, left[q, 0], left[q, 1])

    def top_entry(b):
        rows, half = n // 2, order // 2
        last = order_ref[order_ref.shape[0] - 1]
        at = pl.ds(core * rows, rows)
        value = slices_ref[b]
        top_real, top_imag = complex_rows(
            middle[b][last, 0, at].reshape(half, width),
            middle[b][last, 1, at].reshape(half, width),
            middle[b][1 - last, 0].reshape(order, width),
            middle[b][1 - last, 1].reshape(order, width),
        )
        real_part, imag_part = complex_rows(
            top_real.astype(prod.dtype),
            top_imag.astype(prod.dtype),
            chosen[value, 0],
            chosen[value, 1],
        )
        out_ref[0, b] = real_part
        out_ref[1, b] = imag_part

    boundary_copy = pltpu.make_async_copy(boundary_ref, chosen, chosen_sem)
    for e in range(per):
        leaf_copy(e).start()
    barrier = pltpu.get_barrier_semaphore()
    for k in range(1, n):
        pl.semaphore_signal(
            barrier, inc=1, device_id={"mode": lax.rem(m + k, n)}, device_id_type=MESH
        )
    pl.semaphore_signal(barrier, inc=1, device_id={"branch": 1 - core}, device_id_type=MESH)

    for e in range(per):
        leaf_copy(e).wait()
        first_tile(0, e, 0)
        if e == 0:
            pl.semaphore_wait(barrier, n)
        cross_right(0, e).start()
        for k in range(1, peers):
            column_right(0, e, k, up(k), line).start()
        own_right_copy(0, e).start()
    for e in range(per):
        first_tile(1, e, 0)
        cross_left(0, e).start()
    boundary_copy.start()
    for e in range(per):
        send_relay(0, e)
        later_tiles(0, e)
    for e in range(per):
        later_tiles(1, e)

    moves = {
        "R": send_cross_right,
        "L": send_cross_left,
        "C": send_column,
        "Y": send_relays,
        "Oa": lambda q: send_straight(q, side),
        "Ob": lambda q: send_straight(q, 1 - side),
        "Xa": lambda q: send_crossing(q, side),
        "Xb": lambda q: send_crossing(q, 1 - side),
    }

    def run(steps):
        for move, q in steps:
            moves[move](q)

    outer_steps, inner_steps = schedule(OUTER, rounds), schedule(INNER, rounds)
    for step in range(2 * rounds + 1):
        if outer_steps[step] == inner_steps[step]:
            run(outer_steps[step])
        else:

            @pl.when(outer)
            def _():
                run(outer_steps[step])

            @pl.when(jnp.logical_not(outer))
            def _():
                run(inner_steps[step])

        if step < 2 * rounds:
            (join_across if step % 2 else join_own)(step // 2)

    boundary_copy.wait()
    sources = [(h_from, side_from) for h_from in range(per) for side_from in range(pair)]

    def share(q):
        for h_from, side_from in sources:
            delivered(q, h_from, side_from).wait()
            forward(q, h_from, side_from, core).start()

    mine = [[q for q in range(rounds) if entry(q) == b] for b in range(per)]
    for q in mine[0]:
        share(q)
    for b in range(per):
        for q in mine[b]:
            for h_from, side_from in sources:
                forward(q, h_from, side_from, 1 - core).wait_recv()
        later = mine[b + 1] if b + 1 < per else []
        for q in later[:-1]:
            share(q)
        top_entry(b)
        for q in later[-1:]:
            share(q)

    for q in range(rounds):
        for e in range(per):
            cross_right(q, e).wait_send()
            cross_left(q, e).wait_send()
            for k in range(1, peers):
                column_right(q, e, k, up(k), line).wait_send()
                relay_right(q, e, k, up(k), line).wait_send()
        for i in range(wide):

            @pl.when(wide * line + i != m)
            def _():
                deliver(q, i).wait_send()

        for h_from in range(per):
            for side_from in range(pair):
                forward(q, h_from, side_from, core).wait_send()


def contract(leaves, join_order, slice_values, boundary):
    n = lax.axis_size("mode")
    count, _, per, order, width = leaves.shape
    blk = order // n
    rounds, peers, wide = n // 2, n // per // 2, 2 * per
    dma = pltpu.SemaphoreType.DMA
    dtype = leaves.dtype
    return pl.pallas_call(
        functools.partial(contract_kernel, per),
        out_shape=jax.ShapeDtypeStruct((2, per, order // 2, width), jnp.float32),
        in_specs=[
            pl.BlockSpec(memory_space=pltpu.SMEM),
            pl.BlockSpec(memory_space=pltpu.SMEM),
            pl.BlockSpec(memory_space=pltpu.HBM),
            pl.BlockSpec(memory_space=pltpu.HBM),
        ],
        out_specs=pl.BlockSpec(memory_space=pltpu.VMEM),
        scratch_shapes=[
            pltpu.VMEM((2, 2, per, n, blk, width), dtype),
            pltpu.VMEM((rounds, 2, n, blk, width), dtype),
            pltpu.VMEM((rounds, 2, per, blk, width), dtype),
            pltpu.VMEM((rounds, 2, wide, blk, width), dtype),
            pltpu.VMEM(boundary.shape, dtype),
            dma((per,)),
            dma((rounds, per)),
            dma((rounds, per)),
            dma((rounds, per)),
            dma((rounds, per)),
            dma((rounds, per)),
            dma((rounds, per, peers)),
            dma((rounds, per, peers)),
            dma((rounds, per, peers)),
            dma((rounds, per, peers)),
            dma((rounds, wide)),
            dma((rounds, wide)),
            dma((rounds, wide)),
            dma((rounds, wide)),
            dma(()),
        ]
        + [pltpu.VMEM((count, 2, order, width), dtype)] * per
        + [pltpu.VMEM((2, 2, n, blk, width), dtype)] * per,
        compiler_params=pltpu.CompilerParams(
            collective_id=0, has_side_effects=True, vmem_limit_bytes=48 << 20
        ),
        name="contract",
    )(
        pltpu.with_memory_space_constraint(join_order, pltpu.HBM),
        pltpu.with_memory_space_constraint(slice_values, pltpu.HBM),
        pltpu.with_memory_space_constraint(leaves, pltpu.HBM),
        pltpu.with_memory_space_constraint(boundary, pltpu.HBM),
    )


def per_device(leaves, join_order, slice_values, boundary):
    return contract(leaves, join_order, slice_values, boundary)


def solution(mesh):
    in_specs = (P("branch", None, ("cuts", "mode"), None, None), P(), P(("cuts", "mode")), P())
    out_specs = P(None, ("cuts", "mode"), "branch", None)
    return jax.shard_map(
        per_device, mesh=mesh, in_specs=in_specs, out_specs=out_specs, check_vma=False
    )
```
